512 devices in a mesh: asset: 64 (over y, z), rhs: 8 (over x, core).
Axes of the slice: x: 4, y: 8, z: 8, core: 2. Of those that a mesh axis runs over, the one named last changes fastest.
Arguments:
- targets: float32 [65536, 1024], P('asset', 'rhs'), may hold values from -27 to 27
- ridge: float32 [65536], P('asset'), may hold values from 0.8 to 2.5
- blocks: bfloat16 [512, 16, 128, 128], P('asset', None, 'rhs'), may hold values from -0.046875 to 0.046875
- col_index: int32 [512, 16], P('asset'), may hold values from 0 to 511, as said below
- row_length: int32 [512], P('asset'), may hold values from 8 to 16, as said below
Outputs:
- solution: float32 [65536, 1024], P('asset', 'rhs')
- residual: float32 [65536, 1024], P('asset', 'rhs')
The draws below stay inside these ranges and needn't reach their ends.
Inputs may be any that keep to these rules, and one draw needn't show every extreme that they name: `col_index`: the block columns of row i are distinct and lie within 8 blocks of i, counted cyclically modulo 512; slots at or past row_length[i] hold such columns too and are ignored. `row_length`: each aligned group of 8 block rows holds at least one row with 16 used slots.
All inputs are finite; a program needn't handle non-finite values.
Results may differ from the reference program's by a relative error of at most 0.0075.
Values may be sent and summed in bfloat16 or wider, within the bound.
A program may use at most 64 MiB of HBM per device.

```python
import math
import jax
import jax.numpy as jnp
from jax import lax

BR_DEV = 8
MAXB = 16
BS = 128
ITERS = 3
NB = 512
ASSETS = 65536
RHS = 1024


def draw_targets(key, part):
    key = jax.random.fold_in(key, 31)
    first = jax.random.fold_in(key, 0)
    ramp = (1.0 + 2.0 * jnp.arange(ASSETS, dtype=jnp.float32) / (ASSETS - 1))[:, None]
    values = jnp.clip(jax.random.normal(first, (ASSETS, RHS), jnp.float32), -4.0, 4.0) * ramp
    return values.astype(jnp.float32)


def draw_col_index(key, part):
    key = jax.random.fold_in(key, 17)
    count = 2 * BR_DEV + 1

    def one_row(row):
        order = jax.random.permutation(jax.random.fold_in(key, row), count)
        offsets = order[:MAXB].astype(jnp.int32) - BR_DEV
        return (row + offsets) % NB
    return jax.vmap(one_row)(jnp.arange(NB, dtype=jnp.int32)).astype(jnp.int32)


def draw_row_length(key, part):
    key = jax.random.fold_in(key, 23)
    first, second = jax.random.split(key)
    lengths = jax.random.randint(first, (NB,), MAXB // 2, MAXB + 1)
    picked = jax.random.randint(second, (NB // BR_DEV,), 0, BR_DEV)
    full_row = jnp.arange(NB) % BR_DEV == jnp.repeat(picked, BR_DEV)
    return jnp.where(full_row, MAXB, lengths).astype(jnp.int32)


def levels(rng, shape, cuts, smallest, high):
    loudness = 1.0
    for axis_at, blocks in cuts:
        heights = jax.random.uniform(jax.random.fold_in(jax.random.fold_in(rng, 6), axis_at), (blocks,), jnp.float32, smallest / len(cuts), high / len(cuts))
        loudness = loudness * jnp.repeat(jnp.exp(heights), shape[axis_at] // blocks).reshape((-1,) + (1,) * (len(shape) - 1 - axis_at))
    return loudness


def centred(key, dims, spread, limit, shards=(), kind=jnp.bfloat16):
    array = jax.random.normal(key, dims, jnp.float32) * spread
    if len(shards) > 0:
        array = levels(key, dims, shards, -0.22, 0.18) * array
    return jnp.clip(array, min=-limit, max=limit).astype(kind)


def setup_inputs(seed: int = 0) -> dict:
    seeds = jax.random.split(jax.random.key(seed), 6)
    targets = draw_targets(jax.random.fold_in(seeds[5], 71), 0)
    ridge = jnp.clip(jnp.exp(math.log(2.5) - 1.13943427 * jax.random.uniform(seeds[1], (ASSETS,), jnp.float32) ** levels(seeds[1], (ASSETS,), ((0, 64),), -0.2, 0.2)), 0.8, 2.5)
    blocks = centred(seeds[2], (NB, MAXB, BS, BS), (8 * MAXB * BS) ** -0.5, 0.046875, ((0, 64), (2, 8)))
    col_index = draw_col_index(jax.random.fold_in(seeds[5], 71), 0)
    row_length = draw_row_length(jax.random.fold_in(seeds[5], 71), 0)
    return {"targets": targets, "ridge": ridge, "blocks": blocks, "col_index": col_index, "row_length": row_length}


def reference(targets, ridge, blocks, col_index, row_length):
    nblocks = blocks.shape[0]
    slots = blocks.shape[1]
    width = blocks.shape[2]
    cols = targets.shape[1]
    used = jnp.arange(slots)[None, :] < row_length[:, None]
    masked = blocks * used[:, :, None, None].astype(jnp.bfloat16)

    def operate(field):
        rounded = lax.optimization_barrier(field.astype(jnp.bfloat16))
        vt = rounded.astype(jnp.float32).reshape(nblocks, width, cols)

        def forward_row(item):
            block_set, index = item
            return jnp.einsum('kab,kbn->an', block_set.astype(jnp.float32), vt[index],
                              precision=lax.Precision.HIGHEST)

        forward = lax.map(forward_row, (masked, col_index))

        def back_step(carry, item):
            block_set, index, row_vals = item
            part = jnp.einsum('kab,an->kbn', block_set.astype(jnp.float32), row_vals,
                              precision=lax.Precision.HIGHEST)
            return carry.at[index].add(part), None

        backward, unused = lax.scan(back_step, jnp.zeros((nblocks, width, cols), jnp.float32),
                                    (masked, col_index, vt))
        return ridge[:, None] * field + 0.5 * (forward + backward).reshape(nblocks * width, cols)

    solution = jnp.zeros_like(targets)
    residual = targets
    direction = targets
    norm_now = jnp.sum(residual * residual, axis=0)
    for step in range(ITERS):
        image = operate(direction)
        alpha = norm_now / jnp.sum(direction * image, axis=0)
        solution = solution + alpha * direction
        residual = residual - alpha * image
        norm_next = jnp.sum(residual * residual, axis=0)
        direction = residual + (norm_next / norm_now) * direction
        norm_now = norm_next
    return solution, residual
```

```python
import functools

import jax
import jax.numpy as jnp
from jax import lax
from jax.experimental import pallas as pl
from jax.experimental.pallas import tpu as pltpu
from jax.sharding import PartitionSpec as P

ITERS = 3
ROWS = 8
BAND = 2 * ROWS + 1
BS = 128
PAIRS = ROWS // 2
CHUNK = 2 * BAND
SIDE = ROWS + 1
UP_AT = ROWS
DN_AT = CHUNK - SIDE
OWN = PAIRS * CHUNK
PREV_AT = OWN
NEXT_AT = OWN + PAIRS * SIDE
TILES = OWN + 2 * PAIRS * SIDE
PARTS = 8
SUB = BS // PARTS
NX = 4
RING = 8
MESH = pl.DeviceIdType.MESH


def place(row, c):
    low = (c - ROWS + row + CHUNK) % CHUNK
    high = 3 * ROWS + 1 + (ROWS - 1 - row) - c
    pair = jnp.where(row < PAIRS, row, ROWS - 1 - row)
    return pair, jnp.where(row < PAIRS, low, high)


def lanes(tile, count):
    return pl.ds(pl.multiple_of(tile * BS, BS), count * BS)


def kernel(
    pick_ref, mask_ref, targets_ref, ridge_ref, blocks_ref,
    sol_ref, res_ref,
    stored, tiles, band, vec, acc, d, q, w, ridge, red_out, red_in,
    load_sem, send_sem, recv_sem, halo_send, halo_recv, red_send, red_recv,
):
    asset = lax.axis_index("asset")
    part = lax.axis_index("rhs")
    assets = lax.axis_size("asset")
    y, z = asset // RING, asset % RING
    x, core = part // 2, part % 2

    def at_x(step):
        return ((x + step) % NX) * 2 + core

    right, left, far = at_x(1), at_x(NX - 1), at_x(2)
    mate = x * 2 + (1 - core)
    following = (asset + 1) % assets
    preceding = (asset + assets - 1) % assets

    def z_peer(step):
        return y * RING + (z + step) % RING

    def y_peer(step):
        return ((y + step) % RING) * RING + z

    load_blocks = pltpu.make_async_copy(blocks_ref, stored, load_sem.at[0])
    load_targets = pltpu.make_async_copy(targets_ref, res_ref, load_sem.at[1])
    load_blocks.start()
    load_targets.start()

    barrier = pltpu.get_barrier_semaphore()
    greet = [{"rhs": r} for r in (right, left, mate)]
    greet += [{"asset": a} for a in (following, preceding)]
    for step in range(1, RING):
        greet += [{"asset": z_peer(step)}, {"asset": y_peer(step)}]
    for device in greet:
        pl.semaphore_signal(barrier, inc=1, device_id=device, device_id_type=MESH)
    pl.semaphore_wait(barrier, len(greet))

    sent = []

    def copy(index, sems, src, dst, device):
        return pltpu.make_async_remote_copy(
            src_ref=src, dst_ref=dst, send_sem=sems[0].at[index], recv_sem=sems[1].at[index],
            device_id=device, device_id_type=MESH,
        )

    gather = (send_sem, recv_sem)
    KINDS = 23

    def slab(shard, first, count):
        return tiles.at[shard, :, lanes(first, count)]

    def tile_copy(g, kind, shard, first, count, device, to=None):
        to = first if to is None else to
        return copy(g * KINDS + kind, gather, slab(shard, first, count), slab(shard, to, count), device)

    def launch(one):
        one.start()
        sent.append(one)

    def spread(g, source, shard):
        launch(tile_copy(g, 3 + source, shard, g * CHUNK, CHUNK, {"rhs": mate}))
        launch(tile_copy(g, 7 + source, shard, g * CHUNK + UP_AT, SIDE, {"asset": following}, PREV_AT + g * SIDE))
        launch(tile_copy(g, 11 + source, shard, g * CHUNK + DN_AT, SIDE, {"asset": preceding}, NEXT_AT + g * SIDE))

    def land(g, kind, shard, first, count):
        tile_copy(g, kind, shard, first, count, {"rhs": mate}).wait_recv()

    def from_left(g):
        land(g, 0, left, g * CHUNK, CHUNK)
        if g % 2 == 0:
            launch(tile_copy(g, 2, left, g * CHUNK, CHUNK, {"rhs": right}))
        spread(g, 1, left)

    def from_right(g):
        land(g, 1, right, g * CHUNK, CHUNK)
        if g % 2 == 1:
            launch(tile_copy(g, 2, right, g * CHUNK, CHUNK, {"rhs": left}))
        spread(g, 2, right)

    def from_far(g):
        land(g, 2, far, g * CHUNK, CHUNK)
        spread(g, 3, far)

    shards = (part, left, right, far)

    def from_sides(g, source):
        shard = shards[source]
        land(g, 7 + source, shard, PREV_AT + g * SIDE, SIDE)
        launch(tile_copy(g, 15 + source, shard, PREV_AT + g * SIDE, SIDE, {"rhs": mate}))
        land(g, 11 + source, shard, NEXT_AT + g * SIDE, SIDE)
        launch(tile_copy(g, 19 + source, shard, NEXT_AT + g * SIDE, SIDE, {"rhs": mate}))

    def mate_shard(source):
        return ((x + (0, NX - 1, 1, 2)[source]) % NX) * 2 + (1 - core)

    load_blocks.wait()
    for g in range(PAIRS):
        for row in (g, ROWS - 1 - g):

            def densify(c, unused, row=row, g=g):
                pair, at = place(jnp.int32(row), c)
                block = stored[row, pick_ref[row, c]].astype(jnp.float32)
                tiles[part, :, lanes(g * CHUNK + at, 1)] = (block * mask_ref[row, c]).astype(jnp.bfloat16)
                return unused

            lax.fori_loop(0, BAND, densify, 0)
        launch(tile_copy(g, 0, part, g * CHUNK, CHUNK, {"rhs": right}))
        launch(tile_copy(g, 1, part, g * CHUNK, CHUNK, {"rhs": left}))
        spread(g, 0, part)

    def rows(t):
        return pl.ds(pl.multiple_of(t * BS, BS), BS)

    def middle(t):
        return pl.ds(pl.multiple_of((ROWS + t) * BS, BS), BS)

    def halo(step, side):
        length = ROWS * BS
        return copy(
            2 * step + side, (halo_send, halo_recv),
            vec.at[step, pl.ds(length, length), :],
            vec.at[step, pl.ds(2 * length * side, length), :],
            {"asset": (following, preceding)[side]},
        )

    load_targets.wait()

    def round_targets(t, unused):
        vec[0, middle(t), :] = res_ref[rows(t), :].astype(jnp.bfloat16)
        return unused

    lax.fori_loop(0, ROWS, round_targets, 0)
    for side in range(2):
        launch(halo(0, side))

    def spread_ridge(t, unused):
        ridge[rows(t), :] = jnp.broadcast_to(ridge_ref[pl.ds(t, 1), :], (BS, BS)).T
        return unused

    lax.fori_loop(0, ROWS, spread_ridge, 0)

    for g in range(PAIRS):
        from_left(g)
        from_right(g)
        from_sides(g, 0)
        if g >= 1:
            from_far(g - 1)
            from_sides(g - 1, 1)
            from_sides(g - 1, 2)
    from_far(PAIRS - 1)
    from_sides(PAIRS - 1, 1)
    from_sides(PAIRS - 1, 2)
    for g in range(PAIRS):
        from_sides(g, 3)
    for g in range(PAIRS):
        for source in range(4):
            shard = mate_shard(source)
            land(g, 3 + source, shard, g * CHUNK, CHUNK)
            land(g, 15 + source, shard, PREV_AT + g * SIDE, SIDE)
            land(g, 19 + source, shard, NEXT_AT + g * SIDE, SIDE)

    def tile(index):
        return tiles[:, :, lanes(index, 1)].reshape(BS, BS)

    def weave(t, unused):
        def one(c, unused):
            pair, at = place(t, c)
            source = t + c
            row = source % ROWS
            pair_t, at_t = place(row, BAND - 1 - c)
            index = jnp.where(
                source < ROWS,
                PREV_AT + pair_t * SIDE + at_t - UP_AT,
                jnp.where(
                    source < 2 * ROWS,
                    pair_t * CHUNK + at_t,
                    NEXT_AT + pair_t * SIDE + at_t - DN_AT,
                ),
            )
            band[t, :, lanes(t + c, 1)] = tile(pair * CHUNK + at) + tile(index).T
            return unused

        return lax.fori_loop(0, BAND, one, unused)

    lax.fori_loop(0, ROWS, weave, 0)

    def multiply(step, side):
        span = ROWS * BS
        field = vec.at[step, pl.ds(side * span, span), :]
        for t in range(ROWS):
            if side == 0:
                low, high = t, ROWS
            elif side == 1:
                low, high = 0, ROWS
            else:
                low, high = 0, t + 1
            product = jnp.dot(
                band[t, :, side * span + low * BS : side * span + high * BS],
                field[low * BS : high * BS, :],
                preferred_element_type=jnp.float32,
            )
            if side == 1:
                acc[rows(t), :] = product
            else:
                acc[rows(t), :] += product

    def fold(values):
        return jnp.sum(values.reshape(BS // 8, 8, BS), axis=0)

    def total(step, values):
        for phase in range(2):
            red_out[2 * step + phase] = values
            peer = (z_peer, y_peer)[phase]
            base = (2 * step + phase) * (RING - 1)
            copies = [
                copy(base + hop - 1, (red_send, red_recv), red_out.at[2 * step + phase],
                     red_in.at[base + hop - 1], {"asset": peer(hop)})
                for hop in range(1, RING)
            ]
            for one in copies:
                launch(one)
            for one in copies:
                one.wait_recv()
            for hop in range(1, RING):
                values = values + red_in[base + hop - 1]
        return values

    before, curve_before = None, None
    for step in range(ITERS):
        multiply(step, 1)
        for side in range(2):
            halo(step, side).wait_recv()
        multiply(step, 0)
        multiply(step, 2)

        def dots(t, sums, step=step):
            r = res_ref[rows(t), :]
            wt = ridge[rows(t), :] * r + 0.5 * acc[rows(t), :]
            w[rows(t), :] = wt
            out = [sums[0] + fold(r * r), sums[1] + fold(r * wt)]
            if step > 0:
                out.append(sums[2] + fold(r * q[rows(t), :] + d[rows(t), :] * wt))
            return tuple(out)

        count = 2 if step == 0 else 3
        sums = lax.fori_loop(0, ROWS, dots, (jnp.zeros((8, BS), jnp.float32),) * count)
        line = lax.broadcasted_iota(jnp.int32, (8, BS), 0)
        packed = jnp.zeros((8, BS), jnp.float32)
        for i in range(count):
            packed = jnp.where(line == i, jnp.sum(sums[i], axis=0, keepdims=True), packed)
        packed = total(step, packed)
        norm, curve = packed[0:1, :], packed[1:2, :]
        if step > 0:
            beta = norm / before
            curve = curve + beta * (packed[2:3, :] + beta * curve_before)
        alpha = norm / curve
        before, curve_before = norm, curve

        def update(t, unused, step=step):
            r = res_ref[rows(t), :]
            dt, qt = r, w[rows(t), :]
            if step > 0:
                dt = dt + beta * d[rows(t), :]
                qt = qt + beta * q[rows(t), :]
            moved = alpha * dt
            sol_ref[rows(t), :] = moved if step == 0 else sol_ref[rows(t), :] + moved
            r = r - alpha * qt
            res_ref[rows(t), :] = r
            if step < ITERS - 1:
                d[rows(t), :] = dt
                q[rows(t), :] = qt
                vec[step + 1, middle(t), :] = r.astype(jnp.bfloat16)
            return unused

        lax.fori_loop(0, ROWS, update, 0)
        if step < ITERS - 1:
            for side in range(2):
                launch(halo(step + 1, side))

    for one in sent:
        one.wait_send()


def local(targets, ridge, blocks, col_index, row_length):
    slots = col_index.shape[1]
    total = ROWS * lax.axis_size("asset")
    start = lax.axis_index("asset") * ROWS
    here = start + jnp.arange(ROWS, dtype=jnp.int32)[:, None]
    offset = (col_index - here + ROWS + total) % total
    used = jnp.arange(slots, dtype=jnp.int32)[None, :] < row_length[:, None]
    hit = (offset[:, None, :] == jnp.arange(BAND, dtype=jnp.int32)[None, :, None]) & used[:, None, :]
    pick = jnp.sum(jnp.where(hit, jnp.arange(slots, dtype=jnp.int32)[None, None, :], 0), axis=2)
    mask = jnp.sum(hit.astype(jnp.float32), axis=2)

    size = ROWS * BS
    f32 = jnp.float32
    vmem = pl.BlockSpec(memory_space=pltpu.VMEM)
    smem = pl.BlockSpec(memory_space=pltpu.SMEM)
    hbm = pl.BlockSpec(memory_space=pl.ANY)
    kinds = PAIRS * 23
    return pl.pallas_call(
        kernel,
        out_shape=[jax.ShapeDtypeStruct((size, BS), f32)] * 2,
        in_specs=[smem, smem, hbm, vmem, hbm],
        out_specs=[vmem, vmem],
        scratch_shapes=[
            pltpu.VMEM((ROWS, slots, SUB, BS), jnp.bfloat16),
            pltpu.VMEM((PARTS, SUB, TILES * BS), jnp.bfloat16),
            pltpu.VMEM((ROWS, BS, 3 * size), jnp.bfloat16),
            pltpu.VMEM((ITERS, 3 * size, BS), jnp.bfloat16),
            pltpu.VMEM((size, BS), f32),
            pltpu.VMEM((size, BS), f32),
            pltpu.VMEM((size, BS), f32),
            pltpu.VMEM((size, BS), f32),
            pltpu.VMEM((size, BS), f32),
            pltpu.VMEM((2 * ITERS, 8, BS), f32),
            pltpu.VMEM((2 * ITERS * (RING - 1), 8, BS), f32),
            pltpu.SemaphoreType.DMA((2,)),
            pltpu.SemaphoreType.DMA((kinds,)),
            pltpu.SemaphoreType.DMA((kinds,)),
            pltpu.SemaphoreType.DMA((2 * ITERS,)),
            pltpu.SemaphoreType.DMA((2 * ITERS,)),
            pltpu.SemaphoreType.DMA((2 * ITERS * (RING - 1),)),
            pltpu.SemaphoreType.DMA((2 * ITERS * (RING - 1),)),
        ],
        compiler_params=pltpu.CompilerParams(
            collective_id=0, has_side_effects=True, vmem_limit_bytes=60 * 2**20
        ),
    )(pick, mask, targets, ridge.reshape(ROWS, BS), blocks)


def solution(mesh):
    return jax.shard_map(
        local,
        mesh=mesh,
        in_specs=(
            P("asset", "rhs"),
            P("asset"),
            P("asset", None, "rhs", None),
            P("asset", None),
            P("asset"),
        ),
        out_specs=(P("asset", "rhs"), P("asset", "rhs")),
        check_vma=False,
    )
```

```python
import functools

import jax
import jax.numpy as jnp
from jax import lax
from jax.experimental import pallas as pl
from jax.experimental.pallas import tpu as pltpu
from jax.sharding import PartitionSpec as P

ITERS = 3
ROWS = 8
BAND = 2 * ROWS + 1
BS = 128
PAIRS = ROWS // 2
CHUNK = 2 * BAND
SIDE = ROWS + 1
UP_AT = ROWS
DN_AT = CHUNK - SIDE
OWN = PAIRS * CHUNK
PREV_AT = OWN
NEXT_AT = OWN + PAIRS * SIDE
TILES = OWN + 2 * PAIRS * SIDE
PARTS = 8
SUB = BS // PARTS
NX = 4
RING = 8
MESH = pl.DeviceIdType.MESH


def place(row, c):
    if row < PAIRS:
        return row, (c - ROWS + row + CHUNK) % CHUNK
    return ROWS - 1 - row, 3 * ROWS + 1 + (ROWS - 1 - row) - c


def lanes(tile, count):
    return pl.ds(pl.multiple_of(tile * BS, BS), count * BS)


def kernel(
    pick_ref, mask_ref, targets_ref, ridge_ref, blocks_ref,
    sol_ref, res_ref,
    stored, tiles, band, vec, acc, d, q, w, ridge, red_out, red_in,
    load_sem, send_sem, recv_sem, halo_send, halo_recv, red_send, red_recv,
):
    asset = lax.axis_index("asset")
    part = lax.axis_index("rhs")
    assets = lax.axis_size("asset")
    y, z = asset // RING, asset % RING
    x, core = part // 2, part % 2

    def at_x(step):
        return ((x + step) % NX) * 2 + core

    right, left, far = at_x(1), at_x(NX - 1), at_x(2)
    mate = x * 2 + (1 - core)
    following = (asset + 1) % assets
    preceding = (asset + assets - 1) % assets

    def z_peer(step):
        return y * RING + (z + step) % RING

    def y_peer(step):
        return ((y + step) % RING) * RING + z

    load_blocks = pltpu.make_async_copy(blocks_ref, stored, load_sem.at[0])
    load_targets = pltpu.make_async_copy(targets_ref, res_ref, load_sem.at[1])
    load_blocks.start()
    load_targets.start()

    barrier = pltpu.get_barrier_semaphore()
    greet = [{"rhs": r} for r in (right, left, mate)]
    greet += [{"asset": a} for a in (following, preceding)]
    for step in range(1, RING):
        greet += [{"asset": z_peer(step)}, {"asset": y_peer(step)}]
    for device in greet:
        pl.semaphore_signal(barrier, inc=1, device_id=device, device_id_type=MESH)
    pl.semaphore_wait(barrier, len(greet))

    sent = []

    def copy(index, sems, src, dst, device):
        return pltpu.make_async_remote_copy(
            src_ref=src, dst_ref=dst, send_sem=sems[0].at[index], recv_sem=sems[1].at[index],
            device_id=device, device_id_type=MESH,
        )

    gather = (send_sem, recv_sem)
    KINDS = 23

    def slab(shard, first, count):
        return tiles.at[shard, :, lanes(first, count)]

    def tile_copy(g, kind, shard, first, count, device, to=None):
        to = first if to is None else to
        return copy(g * KINDS + kind, gather, slab(shard, first, count), slab(shard, to, count), device)

    def launch(one):
        one.start()
        sent.append(one)

    def spread(g, source, shard):
        launch(tile_copy(g, 3 + source, shard, g * CHUNK, CHUNK, {"rhs": mate}))
        launch(tile_copy(g, 7 + source, shard, g * CHUNK + UP_AT, SIDE, {"asset": following}, PREV_AT + g * SIDE))
        launch(tile_copy(g, 11 + source, shard, g * CHUNK + DN_AT, SIDE, {"asset": preceding}, NEXT_AT + g * SIDE))

    def land(g, kind, shard, first, count):
        tile_copy(g, kind, shard, first, count, {"rhs": mate}).wait_recv()

    def from_left(g):
        land(g, 0, left, g * CHUNK, CHUNK)
        if g % 2 == 0:
            launch(tile_copy(g, 2, left, g * CHUNK, CHUNK, {"rhs": right}))
        spread(g, 1, left)

    def from_right(g):
        land(g, 1, right, g * CHUNK, CHUNK)
        if g % 2 == 1:
            launch(tile_copy(g, 2, right, g * CHUNK, CHUNK, {"rhs": left}))
        spread(g, 2, right)

    def from_far(g):
        land(g, 2, far, g * CHUNK, CHUNK)
        spread(g, 3, far)

    shards = (part, left, right, far)

    def from_sides(g, source):
        shard = shards[source]
        land(g, 7 + source, shard, PREV_AT + g * SIDE, SIDE)
        launch(tile_copy(g, 15 + source, shard, PREV_AT + g * SIDE, SIDE, {"rhs": mate}))
        land(g, 11 + source, shard, NEXT_AT + g * SIDE, SIDE)
        launch(tile_copy(g, 19 + source, shard, NEXT_AT + g * SIDE, SIDE, {"rhs": mate}))

    def mate_shard(source):
        return ((x + (0, NX - 1, 1, 2)[source]) % NX) * 2 + (1 - core)

    def densify(g):
        for row in (g, ROWS - 1 - g):

            def one(c, unused, row=row):
                pair, at = place(row, c)
                block = stored[row, pick_ref[row, c]].astype(jnp.float32)
                tiles[part, :, lanes(g * CHUNK + at, 1)] = (block * mask_ref[row, c]).astype(jnp.bfloat16)
                return unused

            lax.fori_loop(0, BAND, one, 0, unroll=True)

    def send_own(g):
        launch(tile_copy(g, 0, part, g * CHUNK, CHUNK, {"rhs": right}))
        launch(tile_copy(g, 1, part, g * CHUNK, CHUNK, {"rhs": left}))

    def rows(t):
        return pl.ds(pl.multiple_of(t * BS, BS), BS)

    def middle(t):
        return pl.ds(pl.multiple_of((ROWS + t) * BS, BS), BS)

    def halo(step, side):
        length = ROWS * BS
        return copy(
            2 * step + side, (halo_send, halo_recv),
            vec.at[step, pl.ds(length, length), :],
            vec.at[step, pl.ds(2 * length * side, length), :],
            {"asset": (following, preceding)[side]},
        )

    load_blocks.wait()
    for g in range(2):
        densify(g)
        send_own(g)
        spread(g, 0, part)

    load_targets.wait()

    def round_targets(t, unused):
        vec[0, middle(t), :] = res_ref[rows(t), :].astype(jnp.bfloat16)
        return unused

    lax.fori_loop(0, ROWS, round_targets, 0)
    for side in range(2):
        launch(halo(0, side))
    for g in range(2, PAIRS):
        densify(g)
        spread(g, 0, part)

    def spread_ridge(t, unused):
        ridge[rows(t), :] = jnp.broadcast_to(ridge_ref[pl.ds(t, 1), :], (BS, BS)).T
        return unused

    lax.fori_loop(0, ROWS, spread_ridge, 0)

    def tile(index):
        return tiles[:, :, lanes(index, 1)].reshape(BS, BS)

    def lay(g):
        for source in range(4):
            land(g, 3 + source, mate_shard(source), g * CHUNK, CHUNK)
        for row in (g, ROWS - 1 - g):

            def one(c, unused, row=row):
                pair, at = place(row, c)
                band[row, :, lanes(row + c, 1)] = tile(g * CHUNK + at)
                return unused

            lax.fori_loop(0, BAND, one, 0, unroll=True)
            acc[row * BS : (row + 1) * BS, :] = whole(row)

    def whole(t):
        return jnp.dot(
            band[t, :, t * BS : (t + BAND) * BS], vec[0, t * BS : (t + BAND) * BS, :],
            preferred_element_type=jnp.float32,
        )

    def fold(values):
        return jnp.sum(values.reshape(BS // 8, 8, BS), axis=0)

    def stack(sums):
        line = lax.broadcasted_iota(jnp.int32, (8, BS), 0)
        packed = jnp.zeros((8, BS), jnp.float32)
        for i, one in enumerate(sums):
            packed = jnp.where(line == i, jnp.sum(one, axis=0, keepdims=True), packed)
        return packed

    def exchange(step, phase):
        peer = (y_peer, z_peer)[phase]
        base = (2 * step + phase) * (RING - 1)
        return [
            copy(base + hop - 1, (red_send, red_recv), red_out.at[2 * step + phase],
                 red_in.at[base + hop - 1], {"asset": peer(hop)})
            for hop in range(1, RING)
        ]

    def start_sum(step, phase, values):
        red_out[2 * step + phase] = values
        for one in exchange(step, phase):
            launch(one)

    def end_sum(step, phase):
        for one in exchange(step, phase):
            one.wait_recv()
        values = red_out[2 * step + phase]
        base = (2 * step + phase) * (RING - 1)
        for hop in range(1, RING):
            values = values + red_in[base + hop - 1]
        return values

    from_left(0)
    send_own(2)
    from_right(0)
    from_left(1)
    send_own(3)
    from_right(1)
    from_sides(0, 0)
    from_sides(1, 0)
    from_left(2)
    from_right(2)
    from_sides(0, 1)
    from_sides(0, 2)
    from_far(0)
    from_left(3)
    from_right(3)
    from_far(1)
    from_sides(2, 0)
    from_sides(3, 0)
    from_sides(1, 1)
    from_sides(1, 2)
    for side in range(2):
        halo(0, side).wait_recv()
    lay(0)
    lay(1)
    from_far(2)
    from_sides(2, 1)
    from_sides(2, 2)
    from_sides(0, 3)
    from_far(3)
    from_sides(1, 3)
    from_sides(3, 1)
    from_sides(3, 2)
    lay(2)
    lay(3)

    def first_dots(t, sums):
        r = res_ref[rows(t), :]
        return sums[0] + fold(r * r), sums[1] + fold(r * (ridge[rows(t), :] * r + acc[rows(t), :]))

    start_sum(0, 0, stack(lax.fori_loop(0, ROWS, first_dots, (jnp.zeros((8, BS), jnp.float32),) * 2)))
    from_sides(2, 3)
    from_sides(3, 3)

    def turn(row, column, index):
        band[row, :, lanes(column, 1)] += tile(index).T

    def mirror(t, unused):
        for source in range(ROWS):
            pair, at = place(source, ROWS + t - source)
            turn(t, ROWS + source, pair * CHUNK + at)
        return unused

    lax.fori_loop(0, ROWS, mirror, 0)
    start_sum(0, 1, end_sum(0, 0))

    for g in range(PAIRS):
        for source in range(4):
            shard = mate_shard(source)
            land(g, 15 + source, shard, PREV_AT + g * SIDE, SIDE)
            land(g, 19 + source, shard, NEXT_AT + g * SIDE, SIDE)
        for m in range(SIDE):
            source, t = (g, m) if m <= g else (ROWS - 1 - g, ROWS - m)
            turn(t, source, PREV_AT + g * SIDE + m)
            source, t = (ROWS - 1 - g, ROWS - 1 - m) if m <= g else (g, m - 1)
            turn(t, 2 * ROWS + source, NEXT_AT + g * SIDE + m)

    def multiply(step, side):
        span = ROWS * BS
        field = vec.at[step, pl.ds(side * span, span), :]
        for t in range(ROWS):
            if side == 0:
                low, high = t, ROWS
            elif side == 1:
                low, high = 0, ROWS
            else:
                low, high = 0, t + 1
            product = jnp.dot(
                band[t, :, side * span + low * BS : side * span + high * BS],
                field[low * BS : high * BS, :],
                preferred_element_type=jnp.float32,
            )
            if side == 1:
                acc[rows(t), :] = product
            else:
                acc[rows(t), :] += product

    before, curve_before = None, None
    for step in range(ITERS):
        if step == 0:
            for t in range(ROWS):
                w[rows(t), :] = ridge[rows(t), :] * res_ref[rows(t), :] + 0.5 * whole(t)
            packed = end_sum(0, 1)
        else:
            multiply(step, 1)
            for side in range(2):
                halo(step, side).wait_recv()
            multiply(step, 0)
            multiply(step, 2)

            def dots(t, sums):
                r = res_ref[rows(t), :]
                wt = ridge[rows(t), :] * r + 0.5 * acc[rows(t), :]
                w[rows(t), :] = wt
                return (
                    sums[0] + fold(r * r),
                    sums[1] + fold(r * wt),
                    sums[2] + fold(r * q[rows(t), :] + d[rows(t), :] * wt),
                )

            start_sum(step, 0, stack(lax.fori_loop(0, ROWS, dots, (jnp.zeros((8, BS), jnp.float32),) * 3)))
            start_sum(step, 1, end_sum(step, 0))
            packed = end_sum(step, 1)
        norm, curve = packed[0:1, :], packed[1:2, :]
        if step > 0:
            beta = norm / before
            curve = curve + beta * (packed[2:3, :] + beta * curve_before)
        alpha = norm / curve
        before, curve_before = norm, curve

        def update(t, unused, step=step):
            r = res_ref[rows(t), :]
            dt, qt = r, w[rows(t), :]
            if step > 0:
                dt = dt + beta * d[rows(t), :]
                qt = qt + beta * q[rows(t), :]
            moved = alpha * dt
            sol_ref[rows(t), :] = moved if step == 0 else sol_ref[rows(t), :] + moved
            r = r - alpha * qt
            res_ref[rows(t), :] = r
            if step < ITERS - 1:
                d[rows(t), :] = dt
                q[rows(t), :] = qt
                vec[step + 1, middle(t), :] = r.astype(jnp.bfloat16)
            return unused

        lax.fori_loop(0, ROWS, update, 0)
        if step < ITERS - 1:
            for side in range(2):
                launch(halo(step + 1, side))

    for one in sent:
        one.wait_send()


def local(targets, ridge, blocks, col_index, row_length):
    slots = col_index.shape[1]
    total = ROWS * lax.axis_size("asset")
    start = lax.axis_index("asset") * ROWS
    here = start + jnp.arange(ROWS, dtype=jnp.int32)[:, None]
    offset = (col_index - here + ROWS + total) % total
    used = jnp.arange(slots, dtype=jnp.int32)[None, :] < row_length[:, None]
    hit = (offset[:, None, :] == jnp.arange(BAND, dtype=jnp.int32)[None, :, None]) & used[:, None, :]
    pick = jnp.sum(jnp.where(hit, jnp.arange(slots, dtype=jnp.int32)[None, None, :], 0), axis=2)
    mask = jnp.sum(hit.astype(jnp.float32), axis=2)

    size = ROWS * BS
    f32 = jnp.float32
    vmem = pl.BlockSpec(memory_space=pltpu.VMEM)
    smem = pl.BlockSpec(memory_space=pltpu.SMEM)
    hbm = pl.BlockSpec(memory_space=pl.ANY)
    kinds = PAIRS * 23
    return pl.pallas_call(
        kernel,
        out_shape=[jax.ShapeDtypeStruct((size, BS), f32)] * 2,
        in_specs=[smem, smem, hbm, vmem, hbm],
        out_specs=[vmem, vmem],
        scratch_shapes=[
            pltpu.VMEM((ROWS, slots, SUB, BS), jnp.bfloat16),
            pltpu.VMEM((PARTS, SUB, TILES * BS), jnp.bfloat16),
            pltpu.VMEM((ROWS, BS, 3 * size), jnp.bfloat16),
            pltpu.VMEM((ITERS, 3 * size, BS), jnp.bfloat16),
            pltpu.VMEM((size, BS), f32),
            pltpu.VMEM((size, BS), f32),
            pltpu.VMEM((size, BS), f32),
            pltpu.VMEM((size, BS), f32),
            pltpu.VMEM((size, BS), f32),
            pltpu.VMEM((2 * ITERS, 8, BS), f32),
            pltpu.VMEM((2 * ITERS * (RING - 1), 8, BS), f32),
            pltpu.SemaphoreType.DMA((2,)),
            pltpu.SemaphoreType.DMA((kinds,)),
            pltpu.SemaphoreType.DMA((kinds,)),
            pltpu.SemaphoreType.DMA((2 * ITERS,)),
            pltpu.SemaphoreType.DMA((2 * ITERS,)),
            pltpu.SemaphoreType.DMA((2 * ITERS * (RING - 1),)),
            pltpu.SemaphoreType.DMA((2 * ITERS * (RING - 1),)),
        ],
        compiler_params=pltpu.CompilerParams(
            collective_id=0, has_side_effects=True, vmem_limit_bytes=60 * 2**20
        ),
    )(pick, mask, targets, ridge.reshape(ROWS, BS), blocks)


def solution(mesh):
    return jax.shard_map(
        local,
        mesh=mesh,
        in_specs=(
            P("asset", "rhs"),
            P("asset"),
            P("asset", None, "rhs", None),
            P("asset", None),
            P("asset"),
        ),
        out_specs=(P("asset", "rhs"), P("asset", "rhs")),
        check_vma=False,
    )
```

```python
import functools

import jax
import jax.numpy as jnp
from jax import lax
from jax.experimental import pallas as pl
from jax.experimental.pallas import tpu as pltpu
from jax.sharding import PartitionSpec as P

ITERS = 3
ROWS = 8
BAND = 2 * ROWS + 1
BS = 128
PAIRS = ROWS // 2
CHUNK = 2 * BAND
SIDE = ROWS + 1
UP_AT = ROWS
DN_AT = CHUNK - SIDE
OWN = PAIRS * CHUNK
PREV_AT = OWN
NEXT_AT = OWN + PAIRS * SIDE
TILES = OWN + 2 * PAIRS * SIDE
PIECE = 2
PIECES = ROWS // PIECE
PARTS = 8
SUB = BS // PARTS
NX = 4
RING = 8
MESH = pl.DeviceIdType.MESH


def place(row, c):
    if row < PAIRS:
        return row, (c - ROWS + row + CHUNK) % CHUNK
    return ROWS - 1 - row, 3 * ROWS + 1 + (ROWS - 1 - row) - c


def lanes(tile, count):
    return pl.ds(pl.multiple_of(tile * BS, BS), count * BS)


def kernel(
    col_ref, length_ref, targets_ref, ridge_ref, blocks_ref,
    sol_ref, res_ref, d, q, w, coef_ref,
    col, length, slot, stored, tiles, band, vec, acc, ridge_rows, ridge, red_out, red_in,
    load_sem, send_sem, recv_sem, halo_send, halo_recv, red_send, red_recv,
):
    asset = lax.axis_index("asset")
    part = lax.axis_index("rhs")
    assets = lax.axis_size("asset")
    y, z = asset // RING, asset % RING
    x, core = part // 2, part % 2

    def at_x(step):
        return ((x + step) % NX) * 2 + core

    right, left, far = at_x(1), at_x(NX - 1), at_x(2)
    mate = x * 2 + (1 - core)
    following = (asset + 1) % assets
    preceding = (asset + assets - 1) % assets

    def z_peer(step):
        return y * RING + (z + step) % RING

    def y_peer(step):
        return ((y + step) % RING) * RING + z

    load_blocks = pltpu.make_async_copy(blocks_ref, stored, load_sem.at[0])
    load_targets = pltpu.make_async_copy(targets_ref, res_ref, load_sem.at[1])
    load_col = pltpu.make_async_copy(col_ref, col, load_sem.at[2])
    load_length = pltpu.make_async_copy(length_ref, length, load_sem.at[3])
    load_ridge = pltpu.make_async_copy(ridge_ref, ridge_rows, load_sem.at[4])
    load_col.start()
    load_length.start()
    load_blocks.start()
    load_targets.start()
    load_ridge.start()

    barrier = pltpu.get_barrier_semaphore()
    greet = [{"rhs": r} for r in (right, left, mate)]
    greet += [{"asset": a} for a in (following, preceding)]
    for step in range(1, RING):
        greet += [{"asset": z_peer(step)}, {"asset": y_peer(step)}]
    for device in greet:
        pl.semaphore_signal(barrier, inc=1, device_id=device, device_id_type=MESH)

    load_col.wait()
    load_length.wait()
    slots = col.shape[1]
    blocks_in_all = assets * ROWS

    def find(row, unused):
        here = asset * ROWS + row - ROWS
        offsets = []
        for k in range(slots):
            offset = col[row, k] - here
            offset = jnp.where(offset < 0, offset + blocks_in_all, offset)
            offset = jnp.where(offset >= blocks_in_all, offset - blocks_in_all, offset)
            offsets.append(jnp.where(k < length[row], offset, -1))
        for c in range(BAND):
            found = jnp.int32(0)
            for k in range(slots):
                found = jnp.where(offsets[k] == c, k + 1, found)
            slot[row, c] = found
        return unused

    lax.fori_loop(0, ROWS, find, 0)
    pl.semaphore_wait(barrier, len(greet))

    sent = []

    def copy(index, sems, src, dst, device):
        return pltpu.make_async_remote_copy(
            src_ref=src, dst_ref=dst, send_sem=sems[0].at[index], recv_sem=sems[1].at[index],
            device_id=device, device_id_type=MESH,
        )

    gather = (send_sem, recv_sem)
    KINDS = 23

    def slab(shard, first, count):
        return tiles.at[shard, :, lanes(first, count)]

    def tile_copy(g, kind, shard, first, count, device, to=None):
        to = first if to is None else to
        return copy(g * KINDS + kind, gather, slab(shard, first, count), slab(shard, to, count), device)

    def launch(one):
        one.start()
        sent.append(one)

    def spread(g, source, shard):
        launch(tile_copy(g, 3 + source, shard, g * CHUNK, CHUNK, {"rhs": mate}))
        launch(tile_copy(g, 7 + source, shard, g * CHUNK + UP_AT, SIDE, {"asset": following}, PREV_AT + g * SIDE))
        launch(tile_copy(g, 11 + source, shard, g * CHUNK + DN_AT, SIDE, {"asset": preceding}, NEXT_AT + g * SIDE))

    def land(g, kind, shard, first, count):
        tile_copy(g, kind, shard, first, count, {"rhs": mate}).wait_recv()

    def from_left(g):
        land(g, 0, left, g * CHUNK, CHUNK)
        if g % 2 == 0:
            launch(tile_copy(g, 2, left, g * CHUNK, CHUNK, {"rhs": right}))
        spread(g, 1, left)

    def from_right(g):
        land(g, 1, right, g * CHUNK, CHUNK)
        if g % 2 == 1:
            launch(tile_copy(g, 2, right, g * CHUNK, CHUNK, {"rhs": left}))
        spread(g, 2, right)

    def from_far(g):
        land(g, 2, far, g * CHUNK, CHUNK)
        spread(g, 3, far)

    shards = (part, left, right, far)

    def from_sides(g, source):
        shard = shards[source]
        land(g, 7 + source, shard, PREV_AT + g * SIDE, SIDE)
        launch(tile_copy(g, 15 + source, shard, PREV_AT + g * SIDE, SIDE, {"rhs": mate}))
        land(g, 11 + source, shard, NEXT_AT + g * SIDE, SIDE)
        launch(tile_copy(g, 19 + source, shard, NEXT_AT + g * SIDE, SIDE, {"rhs": mate}))

    def mate_shard(source):
        return ((x + (0, NX - 1, 1, 2)[source]) % NX) * 2 + (1 - core)

    def densify(g):
        for row in (g, ROWS - 1 - g):

            def one(c, unused, row=row):
                pair, at = place(row, c)
                found = slot[row, c]
                block = stored[row, jnp.maximum(found - 1, 0)].astype(jnp.float32)
                keep = jnp.minimum(found, 1).astype(jnp.float32)
                tiles[part, :, lanes(g * CHUNK + at, 1)] = (block * keep).astype(jnp.bfloat16)
                return unused

            lax.fori_loop(0, BAND, one, 0, unroll=True)

    def send_own(g):
        launch(tile_copy(g, 0, part, g * CHUNK, CHUNK, {"rhs": right}))
        launch(tile_copy(g, 1, part, g * CHUNK, CHUNK, {"rhs": left}))

    def rows(t):
        return pl.ds(pl.multiple_of(t * BS, BS), BS)

    def middle(t):
        return pl.ds(pl.multiple_of((ROWS + t) * BS, BS), BS)

    def halo(step, side, piece):
        span, at = ROWS * BS, piece * PIECE * BS
        return copy(
            (2 * step + side) * PIECES + piece, (halo_send, halo_recv),
            vec.at[step, pl.ds(span + at, PIECE * BS), :],
            vec.at[step, pl.ds(2 * span * side + at, PIECE * BS), :],
            {"asset": (following, preceding)[side]},
        )

    load_blocks.wait()
    for g in range(2):
        densify(g)
        send_own(g)
        spread(g, 0, part)

    load_targets.wait()

    def round_targets(t, unused):
        vec[0, middle(t), :] = res_ref[rows(t), :].astype(jnp.bfloat16)
        return unused

    lax.fori_loop(0, ROWS, round_targets, 0)
    for piece in range(PIECES):
        for side in range(2):
            launch(halo(0, side, piece))
    for g in range(2, PAIRS):
        densify(g)
        spread(g, 0, part)

    def spread_ridge(t, unused):
        ridge[rows(t), :] = jnp.broadcast_to(ridge_rows[pl.ds(t, 1), :], (BS, BS)).T
        return unused

    load_ridge.wait()
    lax.fori_loop(0, ROWS, spread_ridge, 0)
    for t in range(0, ROWS, PIECE):
        for low in range(PIECE):
            for high in range(low + 1, PIECE):
                band[t + high, :, lanes(t + low, 1)] = jnp.zeros((BS, BS), jnp.bfloat16)
                band[t + low, :, lanes(2 * ROWS + t + high, 1)] = jnp.zeros((BS, BS), jnp.bfloat16)

    def tile(index):
        return tiles[:, :, lanes(index, 1)].reshape(BS, BS)

    def lay(g):
        for source in range(4):
            land(g, 3 + source, mate_shard(source), g * CHUNK, CHUNK)
        for row in (g, ROWS - 1 - g):

            def one(c, unused, row=row):
                pair, at = place(row, c)
                band[row, :, lanes(row + c, 1)] = tile(g * CHUNK + at)
                return unused

            lax.fori_loop(0, BAND, one, 0, unroll=True)
            acc[row * BS : (row + 1) * BS, :] = whole(row)

    def whole(t):
        return jnp.dot(
            band[t, :, t * BS : (t + BAND) * BS], vec[0, t * BS : (t + BAND) * BS, :],
            preferred_element_type=jnp.float32,
        )

    def fold(values):
        return jnp.sum(values.reshape(BS // 8, 8, BS), axis=0)

    def stack(sums):
        line = lax.broadcasted_iota(jnp.int32, (8, BS), 0)
        packed = jnp.zeros((8, BS), jnp.float32)
        for i, one in enumerate(sums):
            packed = jnp.where(line == i, jnp.sum(one, axis=0, keepdims=True), packed)
        return packed

    def exchange(step, phase):
        peer = (y_peer, z_peer)[phase]
        base = (2 * step + phase) * (RING - 1)
        return [
            copy(base + hop - 1, (red_send, red_recv), red_out.at[2 * step + phase],
                 red_in.at[base + hop - 1], {"asset": peer(hop)})
            for hop in range(1, RING)
        ]

    def start_sum(step, phase, values):
        red_out[2 * step + phase] = values
        for one in exchange(step, phase):
            launch(one)

    def end_sum(step, phase):
        for one in exchange(step, phase):
            one.wait_recv()
        values = red_out[2 * step + phase]
        base = (2 * step + phase) * (RING - 1)
        for hop in range(1, RING):
            values = values + red_in[base + hop - 1]
        return values

    from_left(0)
    send_own(2)
    from_right(0)
    from_left(1)
    send_own(3)
    from_right(1)
    from_sides(0, 0)
    from_sides(1, 0)
    from_left(2)
    from_right(2)
    from_far(0)
    from_left(3)
    from_right(3)
    from_far(1)
    from_sides(2, 0)
    from_sides(3, 0)
    from_sides(0, 1)
    from_sides(0, 2)
    for piece in range(PIECES):
        for side in range(2):
            halo(0, side, piece).wait_recv()
    lay(0)
    lay(1)
    from_far(2)
    from_far(3)
    lay(2)
    lay(3)

    def first_dots(t, sums):
        r = res_ref[rows(t), :]
        return sums[0] + fold(r * r), sums[1] + fold(r * (ridge[rows(t), :] * r + acc[rows(t), :]))

    start_sum(0, 0, stack(lax.fori_loop(0, ROWS, first_dots, (jnp.zeros((8, BS), jnp.float32),) * 2)))
    for g, source in ((1, 1), (1, 2), (2, 1), (2, 2), (0, 3)):
        from_sides(g, source)

    def turn(row, column, index):
        band[row, :, lanes(column, 1)] += tile(index).T

    def mirror(t, unused):
        for source in range(ROWS):
            pair, at = place(source, ROWS + t - source)
            turn(t, ROWS + source, pair * CHUNK + at)
        return unused

    lax.fori_loop(0, PAIRS, mirror, 0)
    for g, source in ((3, 1), (3, 2), (1, 3)):
        from_sides(g, source)
    start_sum(0, 1, end_sum(0, 0))
    for g, source in ((2, 3), (3, 3)):
        from_sides(g, source)
    lax.fori_loop(PAIRS, ROWS, mirror, 0)

    for g in range(PAIRS):
        for source in range(4):
            shard = mate_shard(source)
            land(g, 15 + source, shard, PREV_AT + g * SIDE, SIDE)
            land(g, 19 + source, shard, NEXT_AT + g * SIDE, SIDE)
        for m in range(SIDE):
            source, t = (g, m) if m <= g else (ROWS - 1 - g, ROWS - m)
            turn(t, source, PREV_AT + g * SIDE + m)
            source, t = (ROWS - 1 - g, ROWS - 1 - m) if m <= g else (g, m - 1)
            turn(t, 2 * ROWS + source, NEXT_AT + g * SIDE + m)

    span = ROWS * BS

    def product(step, first, last, column, count):
        left = band[first:last, :, column * BS : (column + count) * BS]
        return jnp.dot(
            left.reshape((last - first) * BS, count * BS), vec[step, column * BS : (column + count) * BS, :],
            preferred_element_type=jnp.float32,
        )

    before, curve_before = None, None
    for step in range(ITERS):
        if step == 0:
            for t in range(ROWS):
                w[rows(t), :] = ridge[rows(t), :] * res_ref[rows(t), :] + 0.5 * whole(t)
            packed = end_sum(0, 1)
        else:
            for t in range(ROWS):
                acc[rows(t), :] = product(step, t, t + 1, ROWS, ROWS)
            for piece in range(PIECES):
                at = piece * PIECE
                halo(step, 0, piece).wait_recv()
                acc[0 : (at + PIECE) * BS, :] += product(step, 0, at + PIECE, at, PIECE)
                halo(step, 1, piece).wait_recv()
                acc[at * BS :, :] += product(step, at, ROWS, 2 * ROWS + at, PIECE)

            def dots(t, sums):
                r = res_ref[rows(t), :]
                wt = ridge[rows(t), :] * r + 0.5 * acc[rows(t), :]
                w[rows(t), :] = wt
                return (
                    sums[0] + fold(r * r),
                    sums[1] + fold(r * wt),
                    sums[2] + fold(r * q[rows(t), :] + d[rows(t), :] * wt),
                )

            start_sum(step, 0, stack(lax.fori_loop(0, ROWS, dots, (jnp.zeros((8, BS), jnp.float32),) * 3)))
            start_sum(step, 1, end_sum(step, 0))
            packed = end_sum(step, 1)
        norm, curve = packed[0:1, :], packed[1:2, :]
        if step > 0:
            beta = norm / before
            curve = curve + beta * (packed[2:3, :] + beta * curve_before)
        alpha = norm / curve
        before, curve_before = norm, curve

        if step == ITERS - 1:
            coef_ref[...] = jnp.concatenate([alpha, beta, jnp.zeros((6, BS), jnp.float32)], axis=0)
            break

        def update(t, unused, step=step):
            r = res_ref[rows(t), :]
            dt, qt = r, w[rows(t), :]
            if step > 0:
                dt = dt + beta * d[rows(t), :]
                qt = qt + beta * q[rows(t), :]
            moved = alpha * dt
            sol_ref[rows(t), :] = moved if step == 0 else sol_ref[rows(t), :] + moved
            r = r - alpha * qt
            res_ref[rows(t), :] = r
            d[rows(t), :] = dt
            q[rows(t), :] = qt
            vec[step + 1, middle(t), :] = r.astype(jnp.bfloat16)
            return unused

        for piece in range(PIECES):
            lax.fori_loop(piece * PIECE, (piece + 1) * PIECE, update, 0)
            for side in range(2):
                launch(halo(step + 1, side, piece))

    for one in sent:
        one.wait_send()


def local(targets, ridge, blocks, col_index, row_length):
    slots = col_index.shape[1]
    size = ROWS * BS
    f32 = jnp.float32
    vmem = pl.BlockSpec(memory_space=pltpu.VMEM)
    hbm = pl.BlockSpec(memory_space=pltpu.HBM)
    kinds = PAIRS * 23
    field = jax.ShapeDtypeStruct((size, BS), f32)
    operands = (col_index, row_length, targets, ridge.reshape(ROWS, BS), blocks)
    solution, residual, d, q, w, coef = pl.pallas_call(
        kernel,
        out_shape=[field] * 5 + [jax.ShapeDtypeStruct((8, BS), f32)],
        in_specs=[hbm] * 5,
        out_specs=[vmem] * 6,
        scratch_shapes=[
            pltpu.SMEM((ROWS, slots), jnp.int32),
            pltpu.SMEM((ROWS,), jnp.int32),
            pltpu.SMEM((ROWS, BAND), jnp.int32),
            pltpu.VMEM((ROWS, slots, SUB, BS), jnp.bfloat16),
            pltpu.VMEM((PARTS, SUB, TILES * BS), jnp.bfloat16),
            pltpu.VMEM((ROWS, BS, 3 * size), jnp.bfloat16),
            pltpu.VMEM((ITERS, 3 * size, BS), jnp.bfloat16),
            pltpu.VMEM((size, BS), f32),
            pltpu.VMEM((ROWS, BS), f32),
            pltpu.VMEM((size, BS), f32),
            pltpu.VMEM((2 * ITERS, 8, BS), f32),
            pltpu.VMEM((2 * ITERS * (RING - 1), 8, BS), f32),
            pltpu.SemaphoreType.DMA((5,)),
            pltpu.SemaphoreType.DMA((kinds,)),
            pltpu.SemaphoreType.DMA((kinds,)),
            pltpu.SemaphoreType.DMA((2 * ITERS * PIECES,)),
            pltpu.SemaphoreType.DMA((2 * ITERS * PIECES,)),
            pltpu.SemaphoreType.DMA((2 * ITERS * (RING - 1),)),
            pltpu.SemaphoreType.DMA((2 * ITERS * (RING - 1),)),
        ],
        compiler_params=pltpu.CompilerParams(
            collective_id=0, has_side_effects=True, vmem_limit_bytes=36 * 2**20
        ),
    )(*(pltpu.with_memory_space_constraint(one, pltpu.HBM) for one in operands))
    alpha, beta = coef[0:1], coef[1:2]
    return solution + alpha * (residual + beta * d), residual - alpha * (w + beta * q)


def solution(mesh):
    return jax.shard_map(
        local,
        mesh=mesh,
        in_specs=(
            P("asset", "rhs"),
            P("asset"),
            P("asset", None, "rhs", None),
            P("asset", None),
            P("asset"),
        ),
        out_specs=(P("asset", "rhs"), P("asset", "rhs")),
        check_vma=False,
    )
```

```python
import functools

import jax
import jax.numpy as jnp
from jax import lax
from jax.experimental import pallas as pl
from jax.experimental.pallas import tpu as pltpu
from jax.sharding import PartitionSpec as P

ITERS = 3
ROWS = 8
BAND = 2 * ROWS + 1
BS = 128
PAIRS = ROWS // 2
CHUNK = 2 * BAND
SIDE = ROWS + 1
UP_AT = ROWS
DN_AT = CHUNK - SIDE
OWN = PAIRS * CHUNK
PREV_AT = OWN
NEXT_AT = OWN + PAIRS * SIDE
TILES = OWN + 2 * PAIRS * SIDE
PIECE = 2
PIECES = ROWS // PIECE
PARTS = 8
SUB = BS // PARTS
NX = 4
RING = 8
MESH = pl.DeviceIdType.MESH


def place(row, c):
    if row < PAIRS:
        return row, (c - ROWS + row + CHUNK) % CHUNK
    return ROWS - 1 - row, 3 * ROWS + 1 + (ROWS - 1 - row) - c


def lanes(tile, count):
    return pl.ds(pl.multiple_of(tile * BS, BS), count * BS)


def kernel(
    col_ref, length_ref, targets_ref, ridge_ref, blocks_ref,
    sol_ref, res_ref, d, q, w, coef_ref,
    col, length, slot, stored, tiles, band, vec, pull, acc, ridge_rows, ridge, red_out, red_in,
    load_sem, send_sem, recv_sem, halo_send, halo_recv, red_send, red_recv,
):
    asset = lax.axis_index("asset")
    part = lax.axis_index("rhs")
    assets = lax.axis_size("asset")
    y, z = asset // RING, asset % RING
    x, core = part // 2, part % 2

    def at_x(step):
        return ((x + step) % NX) * 2 + core

    right, left, far = at_x(1), at_x(NX - 1), at_x(2)
    mate = x * 2 + (1 - core)
    following = (asset + 1) % assets
    preceding = (asset + assets - 1) % assets

    def z_peer(step):
        return y * RING + (z + step) % RING

    def y_peer(step):
        return ((y + step) % RING) * RING + z

    load_blocks = pltpu.make_async_copy(blocks_ref, stored, load_sem.at[0])
    load_targets = pltpu.make_async_copy(targets_ref, res_ref, load_sem.at[1])
    load_col = pltpu.make_async_copy(col_ref, col, load_sem.at[2])
    load_length = pltpu.make_async_copy(length_ref, length, load_sem.at[3])
    load_ridge = pltpu.make_async_copy(ridge_ref, ridge_rows.at[1], load_sem.at[4])
    load_col.start()
    load_length.start()
    load_blocks.start()
    load_targets.start()
    load_ridge.start()

    barrier = pltpu.get_barrier_semaphore()
    greet = [{"rhs": r} for r in (right, left, mate)]
    greet += [{"asset": a} for a in (following, preceding)]
    for step in range(1, RING):
        greet += [{"asset": z_peer(step)}, {"asset": y_peer(step)}]
    for device in greet:
        pl.semaphore_signal(barrier, inc=1, device_id=device, device_id_type=MESH)

    load_col.wait()
    load_length.wait()
    slots = col.shape[1]
    blocks_in_all = assets * ROWS

    def find(row, unused):
        here = asset * ROWS + row - ROWS
        offsets = []
        for k in range(slots):
            offset = col[row, k] - here
            offset = jnp.where(offset < 0, offset + blocks_in_all, offset)
            offset = jnp.where(offset >= blocks_in_all, offset - blocks_in_all, offset)
            offsets.append(jnp.where(k < length[row], offset, -1))
        for c in range(BAND):
            found = jnp.int32(0)
            for k in range(slots):
                found = jnp.where(offsets[k] == c, k + 1, found)
            slot[row, c] = found
        return unused

    lax.fori_loop(0, ROWS, find, 0)
    pl.semaphore_wait(barrier, len(greet))

    sent = []

    def copy(index, sems, src, dst, device):
        return pltpu.make_async_remote_copy(
            src_ref=src, dst_ref=dst, send_sem=sems[0].at[index], recv_sem=sems[1].at[index],
            device_id=device, device_id_type=MESH,
        )

    gather = (send_sem, recv_sem)
    KINDS = 23

    def slab(shard, first, count):
        return tiles.at[shard, :, lanes(first, count)]

    def tile_copy(g, kind, shard, first, count, device, to=None):
        to = first if to is None else to
        return copy(g * KINDS + kind, gather, slab(shard, first, count), slab(shard, to, count), device)

    def launch(one):
        one.start()
        sent.append(one)

    def spread(g, source, shard):
        launch(tile_copy(g, 3 + source, shard, g * CHUNK, CHUNK, {"rhs": mate}))
        launch(tile_copy(g, 7 + source, shard, g * CHUNK + UP_AT, SIDE, {"asset": following}, PREV_AT + g * SIDE))
        launch(tile_copy(g, 11 + source, shard, g * CHUNK + DN_AT, SIDE, {"asset": preceding}, NEXT_AT + g * SIDE))

    def land(g, kind, shard, first, count):
        tile_copy(g, kind, shard, first, count, {"rhs": mate}).wait_recv()

    def from_left(g):
        land(g, 0, left, g * CHUNK, CHUNK)
        if g % 2 == 0:
            launch(tile_copy(g, 2, left, g * CHUNK, CHUNK, {"rhs": right}))
        spread(g, 1, left)

    def from_right(g):
        land(g, 1, right, g * CHUNK, CHUNK)
        if g % 2 == 1:
            launch(tile_copy(g, 2, right, g * CHUNK, CHUNK, {"rhs": left}))
        spread(g, 2, right)

    def from_far(g):
        land(g, 2, far, g * CHUNK, CHUNK)
        spread(g, 3, far)

    shards = (part, left, right, far)

    def from_sides(g, source):
        shard = shards[source]
        land(g, 7 + source, shard, PREV_AT + g * SIDE, SIDE)
        launch(tile_copy(g, 15 + source, shard, PREV_AT + g * SIDE, SIDE, {"rhs": mate}))
        land(g, 11 + source, shard, NEXT_AT + g * SIDE, SIDE)
        launch(tile_copy(g, 19 + source, shard, NEXT_AT + g * SIDE, SIDE, {"rhs": mate}))

    def mate_shard(source):
        return ((x + (0, NX - 1, 1, 2)[source]) % NX) * 2 + (1 - core)

    def densify(g):
        for row in (g, ROWS - 1 - g):

            def one(c, unused, row=row):
                pair, at = place(row, c)
                found = slot[row, c]
                block = stored[row, jnp.maximum(found - 1, 0)].astype(jnp.float32)
                keep = jnp.minimum(found, 1).astype(jnp.float32)
                tiles[part, :, lanes(g * CHUNK + at, 1)] = (block * keep).astype(jnp.bfloat16)
                return unused

            lax.fori_loop(0, BAND, one, 0, unroll=True)

    def send_own(g):
        launch(tile_copy(g, 0, part, g * CHUNK, CHUNK, {"rhs": right}))
        launch(tile_copy(g, 1, part, g * CHUNK, CHUNK, {"rhs": left}))

    def rows(t):
        return pl.ds(pl.multiple_of(t * BS, BS), BS)

    def middle(t):
        return pl.ds(pl.multiple_of((ROWS + t) * BS, BS), BS)

    def halo(step, side, piece):
        span, at = ROWS * BS, piece * PIECE * BS
        field = vec.at[0] if step == 0 else pull.at[step - 1]
        return copy(
            (2 * step + side) * PIECES + piece, (halo_send, halo_recv),
            field.at[pl.ds(span + at, PIECE * BS), :],
            field.at[pl.ds(2 * span * side + at, PIECE * BS), :],
            {"asset": (following, preceding)[side]},
        )

    def ridge_halo(side):
        return copy(
            2 * ITERS * PIECES + side, (halo_send, halo_recv), ridge_rows.at[1], ridge_rows.at[2 * side],
            {"asset": (following, preceding)[side]},
        )

    load_ridge.wait()
    for side in range(2):
        launch(ridge_halo(side))
    load_blocks.wait()
    for g in range(2):
        densify(g)
        send_own(g)
        spread(g, 0, part)

    load_targets.wait()

    def round_targets(t, unused):
        vec[0, middle(t), :] = res_ref[rows(t), :].astype(jnp.bfloat16)
        return unused

    lax.fori_loop(0, ROWS, round_targets, 0)
    for piece in range(PIECES):
        for side in range(2):
            launch(halo(0, side, piece))
    for g in range(2, PAIRS):
        densify(g)
        spread(g, 0, part)

    def spread_ridge(t, unused):
        line = ridge_rows[t // ROWS, pl.ds(t % ROWS, 1), :]
        ridge[rows(t), :] = jnp.broadcast_to(line, (BS, BS)).T
        return unused

    lax.fori_loop(ROWS, 2 * ROWS, spread_ridge, 0)

    def tile(index):
        return tiles[:, :, lanes(index, 1)].reshape(BS, BS)

    def lay(g):
        for source in range(4):
            land(g, 3 + source, mate_shard(source), g * CHUNK, CHUNK)
        for row in (g, ROWS - 1 - g):

            def one(c, unused, row=row):
                pair, at = place(row, c)
                band[row, :, lanes(row + c, 1)] = tile(g * CHUNK + at)
                return unused

            lax.fori_loop(0, BAND, one, 0, unroll=True)
            acc[row * BS : (row + 1) * BS, :] = whole(0, row)

    def whole(step, t):
        return jnp.dot(
            band[t, :, t * BS : (t + BAND) * BS], vec[step, t * BS : (t + BAND) * BS, :],
            preferred_element_type=jnp.float32,
        )

    def fold(values):
        return jnp.sum(values.reshape(BS // 8, 8, BS), axis=0)

    def stack(sums):
        line = lax.broadcasted_iota(jnp.int32, (8, BS), 0)
        packed = jnp.zeros((8, BS), jnp.float32)
        for i, one in enumerate(sums):
            packed = jnp.where(line == i, jnp.sum(one, axis=0, keepdims=True), packed)
        return packed

    def exchange(step, phase):
        peer = ((y_peer, z_peer) if step == 0 else (z_peer, y_peer))[phase]
        base = (2 * step + phase) * (RING - 1)
        return [
            copy(base + hop - 1, (red_send, red_recv), red_out.at[2 * step + phase],
                 red_in.at[base + hop - 1], {"asset": peer(hop)})
            for hop in range(1, RING)
        ]

    def start_sum(step, phase, values):
        red_out[2 * step + phase] = values
        for one in exchange(step, phase):
            launch(one)

    def end_sum(step, phase):
        for one in exchange(step, phase):
            one.wait_recv()
        values = red_out[2 * step + phase]
        base = (2 * step + phase) * (RING - 1)
        for hop in range(1, RING):
            values = values + red_in[base + hop - 1]
        return values

    from_left(0)
    send_own(2)
    from_right(0)
    from_left(1)
    send_own(3)
    from_right(1)
    from_sides(0, 0)
    from_sides(1, 0)
    for side in range(2):
        ridge_halo(side).wait_recv()
    lax.fori_loop(0, ROWS, spread_ridge, 0)
    lax.fori_loop(2 * ROWS, 3 * ROWS, spread_ridge, 0)
    from_left(2)
    from_right(2)
    from_far(0)
    from_left(3)
    from_right(3)
    from_far(1)
    from_sides(2, 0)
    from_sides(3, 0)
    from_sides(0, 1)
    from_sides(0, 2)
    for piece in range(PIECES):
        for side in range(2):
            halo(0, side, piece).wait_recv()
    lay(0)
    lay(1)
    from_far(2)
    from_far(3)
    lay(2)
    lay(3)

    def first_dots(t, sums):
        r = res_ref[rows(t), :]
        return sums[0] + fold(r * r), sums[1] + fold(r * (ridge[middle(t), :] * r + acc[rows(t), :]))

    start_sum(0, 0, stack(lax.fori_loop(0, ROWS, first_dots, (jnp.zeros((8, BS), jnp.float32),) * 2)))
    for g, source in ((1, 1), (1, 2), (2, 1), (2, 2), (0, 3)):
        from_sides(g, source)

    def turn(row, column, index):
        band[row, :, lanes(column, 1)] += tile(index).T

    def mirror(t, unused):
        for source in range(ROWS):
            pair, at = place(source, ROWS + t - source)
            turn(t, ROWS + source, pair * CHUNK + at)
        return unused

    lax.fori_loop(0, PAIRS, mirror, 0)
    for g, source in ((3, 1), (3, 2), (1, 3)):
        from_sides(g, source)
    start_sum(0, 1, end_sum(0, 0))
    for g, source in ((2, 3), (3, 3)):
        from_sides(g, source)
    lax.fori_loop(PAIRS, ROWS, mirror, 0)

    for g in range(PAIRS):
        for source in range(4):
            shard = mate_shard(source)
            land(g, 15 + source, shard, PREV_AT + g * SIDE, SIDE)
            land(g, 19 + source, shard, NEXT_AT + g * SIDE, SIDE)
        for m in range(SIDE):
            source, t = (g, m) if m <= g else (ROWS - 1 - g, ROWS - m)
            turn(t, source, PREV_AT + g * SIDE + m)
            source, t = (ROWS - 1 - g, ROWS - 1 - m) if m <= g else (g, m - 1)
            turn(t, 2 * ROWS + source, NEXT_AT + g * SIDE + m)

    def start_halo(step, piece):
        for side in range(2):
            launch(halo(step, side, piece))

    def end_halo(step):
        for piece in range(PIECES):
            for side in range(2):
                halo(step, side, piece).wait_recv()

    def image(step, t):
        r = res_ref[rows(t), :]
        part_b = 0.5 * whole(step, t)
        wt = ridge[middle(t), :] * r + part_b
        w[rows(t), :] = wt
        if step < ITERS - 1:
            pull[step, middle(t), :] = part_b.astype(jnp.bfloat16)
            if step == 0 and t % PIECE == PIECE - 1:
                start_halo(1, t // PIECE)
        return r, wt

    norms, curves, alphas, betas = [], [], [], [None]
    for step in range(ITERS):
        if step == 0:
            for t in range(ROWS):
                image(0, t)
            packed = end_sum(0, 1)
        else:
            sums = [jnp.zeros((8, BS), jnp.float32)] * 3
            for t in range(ROWS):
                r, wt = image(step, t)
                sums[0] = sums[0] + fold(r * r)
                sums[1] = sums[1] + fold(r * wt)
                sums[2] = sums[2] + fold(r * q[rows(t), :] + d[rows(t), :] * wt)
            start_sum(step, 0, stack(sums))
            early = 2 if step < ITERS - 1 else 0
            for piece in range(early):
                start_halo(step + 1, piece)
            start_sum(step, 1, end_sum(step, 0))
            for piece in range(early, PIECES if step < ITERS - 1 else 0):
                start_halo(step + 1, piece)
            packed = end_sum(step, 1)
        norm, curve = packed[0:1, :], packed[1:2, :]
        if step > 0:
            betas.append(norm / norms[-1])
            curve = curve + betas[-1] * (packed[2:3, :] + betas[-1] * curves[-1])
        norms.append(norm)
        curves.append(curve)
        alphas.append(norm / curve)
        alpha, beta = alphas[-1], betas[-1]
        if step == ITERS - 1:
            coef_ref[...] = jnp.concatenate([alpha, beta, jnp.zeros((6, BS), jnp.float32)], axis=0)
            break

        def update(t, unused, step=step, alpha=alpha, beta=beta):
            r = res_ref[rows(t), :]
            dt, qt = r, w[rows(t), :]
            if step > 0:
                dt = dt + beta * d[rows(t), :]
                qt = qt + beta * q[rows(t), :]
            moved = alpha * dt
            sol_ref[rows(t), :] = moved if step == 0 else sol_ref[rows(t), :] + moved
            r = r - alpha * qt
            res_ref[rows(t), :] = r
            d[rows(t), :] = dt
            q[rows(t), :] = qt
            vec[step + 1, middle(t), :] = r.astype(jnp.bfloat16)
            return unused

        def update_halo(t, unused, step=step):
            for block in (t, 2 * ROWS + t):
                at = rows(block)
                shift = ridge[at, :]
                r = vec[0, at, :].astype(jnp.float32)
                move, push = r, pull[0, at, :].astype(jnp.float32)
                r = r - alphas[0] * (shift * move + push)
                if step > 0:
                    move = r + betas[1] * move
                    push = pull[1, at, :].astype(jnp.float32) + betas[1] * push
                    r = r - alphas[1] * (shift * move + push)
                vec[step + 1, at, :] = r.astype(jnp.bfloat16)
            return unused

        lax.fori_loop(0, ROWS, update, 0)
        end_halo(step + 1)
        lax.fori_loop(0, ROWS, update_halo, 0)

    for one in sent:
        one.wait_send()


def local(targets, ridge, blocks, col_index, row_length):
    slots = col_index.shape[1]
    size = ROWS * BS
    f32 = jnp.float32
    vmem = pl.BlockSpec(memory_space=pltpu.VMEM)
    hbm = pl.BlockSpec(memory_space=pltpu.HBM)
    kinds = PAIRS * 23
    field = jax.ShapeDtypeStruct((size, BS), f32)
    operands = (col_index, row_length, targets, ridge.reshape(ROWS, BS), blocks)
    solution, residual, d, q, w, coef = pl.pallas_call(
        kernel,
        out_shape=[field] * 5 + [jax.ShapeDtypeStruct((8, BS), f32)],
        in_specs=[hbm] * 5,
        out_specs=[vmem] * 6,
        scratch_shapes=[
            pltpu.SMEM((ROWS, slots), jnp.int32),
            pltpu.SMEM((ROWS,), jnp.int32),
            pltpu.SMEM((ROWS, BAND), jnp.int32),
            pltpu.VMEM((ROWS, slots, SUB, BS), jnp.bfloat16),
            pltpu.VMEM((PARTS, SUB, TILES * BS), jnp.bfloat16),
            pltpu.VMEM((ROWS, BS, 3 * size), jnp.bfloat16),
            pltpu.VMEM((ITERS, 3 * size, BS), jnp.bfloat16),
            pltpu.VMEM((ITERS - 1, 3 * size, BS), jnp.bfloat16),
            pltpu.VMEM((size, BS), f32),
            pltpu.VMEM((3, ROWS, BS), f32),
            pltpu.VMEM((3 * size, BS), f32),
            pltpu.VMEM((2 * ITERS, 8, BS), f32),
            pltpu.VMEM((2 * ITERS * (RING - 1), 8, BS), f32),
            pltpu.SemaphoreType.DMA((5,)),
            pltpu.SemaphoreType.DMA((kinds,)),
            pltpu.SemaphoreType.DMA((kinds,)),
            pltpu.SemaphoreType.DMA((2 * ITERS * PIECES + 2,)),
            pltpu.SemaphoreType.DMA((2 * ITERS * PIECES + 2,)),
            pltpu.SemaphoreType.DMA((2 * ITERS * (RING - 1),)),
            pltpu.SemaphoreType.DMA((2 * ITERS * (RING - 1),)),
        ],
        compiler_params=pltpu.CompilerParams(
            collective_id=0, has_side_effects=True, vmem_limit_bytes=36 * 2**20
        ),
    )(*(pltpu.with_memory_space_constraint(one, pltpu.HBM) for one in operands))
    alpha, beta = coef[0:1], coef[1:2]
    return solution + alpha * (residual + beta * d), residual - alpha * (w + beta * q)


def solution(mesh):
    return jax.shard_map(
        local,
        mesh=mesh,
        in_specs=(
            P("asset", "rhs"),
            P("asset"),
            P("asset", None, "rhs", None),
            P("asset", None),
            P("asset"),
        ),
        out_specs=(P("asset", "rhs"), P("asset", "rhs")),
        check_vma=False,
    )
```

```python
import functools

import jax
import jax.numpy as jnp
from jax import lax
from jax.experimental import pallas as pl
from jax.experimental.pallas import tpu as pltpu
from jax.sharding import PartitionSpec as P

ITERS = 3
ROWS = 8
BAND = 2 * ROWS + 1
BS = 128
PAIRS = ROWS // 2
CHUNK = 2 * BAND
SIDE = ROWS + 1
UP_AT = ROWS
DN_AT = CHUNK - SIDE
OWN = PAIRS * CHUNK
PREV_AT = OWN
NEXT_AT = OWN + PAIRS * SIDE
TILES = OWN + 2 * PAIRS * SIDE
PIECE = 2
PIECES = ROWS // PIECE
PARTS = 8
SUB = BS // PARTS
NX = 4
RING = 8
MESH = pl.DeviceIdType.MESH


def place(row, c):
    if row < PAIRS:
        return row, (c - ROWS + row + CHUNK) % CHUNK
    return ROWS - 1 - row, 3 * ROWS + 1 + (ROWS - 1 - row) - c


def lanes(tile, count):
    return pl.ds(pl.multiple_of(tile * BS, BS), count * BS)


def kernel(
    col_ref, length_ref, targets_ref, ridge_ref, blocks_ref,
    sol_ref, res_ref, d, q, w, coef_ref,
    col, length, slot, stored, tiles, band, vec, pull, acc, ridge_rows, ridge, red_out, red_in,
    load_sem, send_sem, recv_sem, halo_send, halo_recv, red_send, red_recv,
):
    asset = lax.axis_index("asset")
    part = lax.axis_index("rhs")
    assets = lax.axis_size("asset")
    y, z = asset // RING, asset % RING
    x, core = part // 2, part % 2

    def at_x(step):
        return ((x + step) % NX) * 2 + core

    right, left, far = at_x(1), at_x(NX - 1), at_x(2)
    mate = x * 2 + (1 - core)
    following = (asset + 1) % assets
    preceding = (asset + assets - 1) % assets

    def z_peer(step):
        return y * RING + (z + step) % RING

    def y_peer(step):
        return ((y + step) % RING) * RING + z

    load_blocks = pltpu.make_async_copy(blocks_ref, stored, load_sem.at[0])
    load_targets = pltpu.make_async_copy(targets_ref, res_ref, load_sem.at[1])
    load_col = pltpu.make_async_copy(col_ref, col, load_sem.at[2])
    load_length = pltpu.make_async_copy(length_ref, length, load_sem.at[3])
    load_ridge = pltpu.make_async_copy(ridge_ref, ridge_rows.at[1], load_sem.at[4])
    load_col.start()
    load_length.start()
    load_blocks.start()
    load_targets.start()
    load_ridge.start()

    barrier = pltpu.get_barrier_semaphore()
    greet = [{"rhs": r} for r in (right, left, mate)]
    greet += [{"asset": a} for a in (following, preceding)]
    for step in range(1, RING):
        greet += [{"asset": z_peer(step)}, {"asset": y_peer(step)}]
    for device in greet:
        pl.semaphore_signal(barrier, inc=1, device_id=device, device_id_type=MESH)

    load_col.wait()
    load_length.wait()
    slots = col.shape[1]
    blocks_in_all = assets * ROWS

    def find(row, unused):
        here = asset * ROWS + row - ROWS
        offsets = []
        for k in range(slots):
            offset = col[row, k] - here
            offset = jnp.where(offset < 0, offset + blocks_in_all, offset)
            offset = jnp.where(offset >= blocks_in_all, offset - blocks_in_all, offset)
            offsets.append(jnp.where(k < length[row], offset, -1))
        for c in range(BAND):
            found = jnp.int32(0)
            for k in range(slots):
                found = jnp.where(offsets[k] == c, k + 1, found)
            slot[row, c] = found
        return unused

    lax.fori_loop(0, ROWS, find, 0)
    pl.semaphore_wait(barrier, len(greet))

    sent = []

    def copy(index, sems, src, dst, device):
        return pltpu.make_async_remote_copy(
            src_ref=src, dst_ref=dst, send_sem=sems[0].at[index], recv_sem=sems[1].at[index],
            device_id=device, device_id_type=MESH,
        )

    gather = (send_sem, recv_sem)
    KINDS = 23

    def slab(shard, first, count):
        return tiles.at[shard, :, lanes(first, count)]

    def tile_copy(g, kind, shard, first, count, device, to=None):
        to = first if to is None else to
        return copy(g * KINDS + kind, gather, slab(shard, first, count), slab(shard, to, count), device)

    def launch(one):
        one.start()
        sent.append(one)

    def spread(g, source, shard):
        launch(tile_copy(g, 3 + source, shard, g * CHUNK, CHUNK, {"rhs": mate}))
        launch(tile_copy(g, 7 + source, shard, g * CHUNK + UP_AT, SIDE, {"asset": following}, PREV_AT + g * SIDE))
        launch(tile_copy(g, 11 + source, shard, g * CHUNK + DN_AT, SIDE, {"asset": preceding}, NEXT_AT + g * SIDE))

    def land(g, kind, shard, first, count):
        tile_copy(g, kind, shard, first, count, {"rhs": mate}).wait_recv()

    def from_left(g):
        land(g, 0, left, g * CHUNK, CHUNK)
        if g % 2 == 0:
            launch(tile_copy(g, 2, left, g * CHUNK, CHUNK, {"rhs": right}))
        spread(g, 1, left)

    def from_right(g):
        land(g, 1, right, g * CHUNK, CHUNK)
        if g % 2 == 1:
            launch(tile_copy(g, 2, right, g * CHUNK, CHUNK, {"rhs": left}))
        spread(g, 2, right)

    def from_far(g):
        land(g, 2, far, g * CHUNK, CHUNK)
        spread(g, 3, far)

    shards = (part, left, right, far)

    def from_sides(g, source):
        shard = shards[source]
        land(g, 7 + source, shard, PREV_AT + g * SIDE, SIDE)
        launch(tile_copy(g, 15 + source, shard, PREV_AT + g * SIDE, SIDE, {"rhs": mate}))
        land(g, 11 + source, shard, NEXT_AT + g * SIDE, SIDE)
        launch(tile_copy(g, 19 + source, shard, NEXT_AT + g * SIDE, SIDE, {"rhs": mate}))

    def mate_shard(source):
        return ((x + (0, NX - 1, 1, 2)[source]) % NX) * 2 + (1 - core)

    def densify(g):
        for row in (g, ROWS - 1 - g):

            def one(c, unused, row=row):
                pair, at = place(row, c)
                found = slot[row, c]
                block = stored[row, jnp.maximum(found - 1, 0)].astype(jnp.float32)
                keep = jnp.minimum(found, 1).astype(jnp.float32)
                tiles[part, :, lanes(g * CHUNK + at, 1)] = (block * keep).astype(jnp.bfloat16)
                return unused

            lax.fori_loop(0, BAND, one, 0, unroll=True)

    def send_own(g):
        launch(tile_copy(g, 0, part, g * CHUNK, CHUNK, {"rhs": right}))
        launch(tile_copy(g, 1, part, g * CHUNK, CHUNK, {"rhs": left}))

    def rows(t):
        return pl.ds(pl.multiple_of(t * BS, BS), BS)

    def middle(t):
        return pl.ds(pl.multiple_of((ROWS + t) * BS, BS), BS)

    def halo(step, side, piece):
        span, at = ROWS * BS, piece * PIECE * BS
        field = vec.at[0] if step == 0 else pull.at[step - 1]
        return copy(
            (2 * step + side) * PIECES + piece, (halo_send, halo_recv),
            field.at[pl.ds(span + at, PIECE * BS), :],
            field.at[pl.ds(2 * span * side + at, PIECE * BS), :],
            {"asset": (following, preceding)[side]},
        )

    def ridge_halo(side):
        return copy(
            2 * ITERS * PIECES + side, (halo_send, halo_recv), ridge_rows.at[1], ridge_rows.at[2 * side],
            {"asset": (following, preceding)[side]},
        )

    load_ridge.wait()
    for side in range(2):
        launch(ridge_halo(side))
    load_blocks.wait()
    for g in range(2):
        densify(g)
        send_own(g)
        spread(g, 0, part)

    load_targets.wait()

    def round_targets(t, unused):
        vec[0, middle(t), :] = res_ref[rows(t), :].astype(jnp.bfloat16)
        return unused

    lax.fori_loop(0, ROWS, round_targets, 0)
    for piece in range(PIECES):
        for side in range(2):
            launch(halo(0, side, piece))
    for g in range(2, PAIRS):
        densify(g)
        send_own(g)
        spread(g, 0, part)

    def spread_ridge(t, unused):
        line = ridge_rows[t // ROWS, pl.ds(t % ROWS, 1), :]
        ridge[rows(t), :] = jnp.broadcast_to(line, (BS, BS)).T
        return unused

    lax.fori_loop(ROWS, 2 * ROWS, spread_ridge, 0)
    for t in range(0, ROWS, 2):
        band[t + 1, :, lanes(t, 1)] = jnp.zeros((BS, BS), jnp.bfloat16)
        band[t, :, lanes(t + BAND, 1)] = jnp.zeros((BS, BS), jnp.bfloat16)

    def tile(index):
        return tiles[:, :, lanes(index, 1)].reshape(BS, BS)

    def lay(g):
        for source in range(4):
            land(g, 3 + source, mate_shard(source), g * CHUNK, CHUNK)
        for row in (g, ROWS - 1 - g):

            def one(c, unused, row=row):
                pair, at = place(row, c)
                band[row, :, lanes(row + c, 1)] = tile(g * CHUNK + at)
                return unused

            lax.fori_loop(0, BAND, one, 0, unroll=True)
            acc[row * BS : (row + 1) * BS, :] = whole(0, row)

    def whole(step, t):
        return jnp.dot(
            band[t, :, t * BS : (t + BAND) * BS], vec[step, t * BS : (t + BAND) * BS, :],
            preferred_element_type=jnp.float32,
        )

    def pair_whole(step, t):
        left = band[t : t + 2, :, t * BS : (t + BAND + 1) * BS].reshape(2 * BS, (BAND + 1) * BS)
        return jnp.dot(
            left, vec[step, t * BS : (t + BAND + 1) * BS, :], preferred_element_type=jnp.float32
        )

    def fold(values):
        return jnp.sum(values.reshape(BS // 8, 8, BS), axis=0)

    def stack(sums):
        line = lax.broadcasted_iota(jnp.int32, (8, BS), 0)
        packed = jnp.zeros((8, BS), jnp.float32)
        for i, one in enumerate(sums):
            packed = jnp.where(line == i, jnp.sum(one, axis=0, keepdims=True), packed)
        return packed

    def exchange(step, phase):
        peer = ((y_peer, z_peer) if step == 0 else (z_peer, y_peer))[phase]
        base = (2 * step + phase) * (RING - 1)
        return [
            copy(base + hop - 1, (red_send, red_recv), red_out.at[2 * step + phase],
                 red_in.at[base + hop - 1], {"asset": peer(hop)})
            for hop in range(1, RING)
        ]

    def start_sum(step, phase, values):
        red_out[2 * step + phase] = values
        for one in exchange(step, phase):
            launch(one)

    def end_sum(step, phase):
        for one in exchange(step, phase):
            one.wait_recv()
        values = red_out[2 * step + phase]
        base = (2 * step + phase) * (RING - 1)
        for hop in range(1, RING):
            values = values + red_in[base + hop - 1]
        return values

    from_left(0)
    from_right(0)
    from_left(1)
    from_right(1)
    from_sides(0, 0)
    from_sides(1, 0)
    for side in range(2):
        ridge_halo(side).wait_recv()
    lax.fori_loop(0, ROWS, spread_ridge, 0)
    lax.fori_loop(2 * ROWS, 3 * ROWS, spread_ridge, 0)
    from_left(2)
    from_right(2)
    from_far(0)
    from_left(3)
    from_right(3)
    from_far(1)
    from_sides(2, 0)
    from_sides(3, 0)
    from_sides(0, 1)
    from_sides(0, 2)
    for piece in range(PIECES):
        for side in range(2):
            halo(0, side, piece).wait_recv()
    lay(0)
    lay(1)
    from_far(2)
    from_far(3)
    lay(2)
    lay(3)

    def first_dots(t, sums):
        r = res_ref[rows(t), :]
        return sums[0] + fold(r * r), sums[1] + fold(r * (ridge[middle(t), :] * r + acc[rows(t), :]))

    start_sum(0, 0, stack(lax.fori_loop(0, ROWS, first_dots, (jnp.zeros((8, BS), jnp.float32),) * 2)))
    for g, source in ((1, 1), (1, 2), (2, 1), (2, 2), (0, 3)):
        from_sides(g, source)

    def turn(row, column, index):
        band[row, :, lanes(column, 1)] += tile(index).T

    def mirror(t, unused):
        for source in range(ROWS):
            pair, at = place(source, ROWS + t - source)
            turn(t, ROWS + source, pair * CHUNK + at)
        return unused

    lax.fori_loop(0, PAIRS, mirror, 0)
    for g, source in ((3, 1), (3, 2), (1, 3)):
        from_sides(g, source)
    start_sum(0, 1, end_sum(0, 0))
    for g, source in ((2, 3), (3, 3)):
        from_sides(g, source)
    lax.fori_loop(PAIRS, ROWS, mirror, 0)

    for g in range(PAIRS):
        for source in range(4):
            shard = mate_shard(source)
            land(g, 15 + source, shard, PREV_AT + g * SIDE, SIDE)
            land(g, 19 + source, shard, NEXT_AT + g * SIDE, SIDE)
        for m in range(SIDE):
            source, t = (g, m) if m <= g else (ROWS - 1 - g, ROWS - m)
            turn(t, source, PREV_AT + g * SIDE + m)
            source, t = (ROWS - 1 - g, ROWS - 1 - m) if m <= g else (g, m - 1)
            turn(t, 2 * ROWS + source, NEXT_AT + g * SIDE + m)

    def start_halo(step, piece):
        for side in range(2):
            launch(halo(step, side, piece))

    def end_halo(step):
        for piece in range(PIECES):
            for side in range(2):
                halo(step, side, piece).wait_recv()

    def image(step, t):
        r = res_ref[rows(t), :]
        if t % 2 == 0:
            acc[t * BS : (t + 2) * BS, :] = 0.5 * pair_whole(step, t)
        part_b = acc[rows(t), :]
        wt = ridge[middle(t), :] * r + part_b
        w[rows(t), :] = wt
        if step < ITERS - 1:
            pull[step, middle(t), :] = part_b.astype(jnp.bfloat16)
            if step == 0 and t % PIECE == PIECE - 1:
                start_halo(1, t // PIECE)
        return r, wt

    norms, curves, alphas, betas = [], [], [], [None]
    for step in range(ITERS):
        if step == 0:
            for t in range(ROWS):
                image(0, t)
            packed = end_sum(0, 1)
        else:
            sums = [jnp.zeros((8, BS), jnp.float32)] * 3
            for t in range(ROWS):
                r, wt = image(step, t)
                sums[0] = sums[0] + fold(r * r)
                sums[1] = sums[1] + fold(r * wt)
                sums[2] = sums[2] + fold(r * q[rows(t), :] + d[rows(t), :] * wt)
            start_sum(step, 0, stack(sums))
            early = 1 if step < ITERS - 1 else 0
            for piece in range(early):
                start_halo(step + 1, piece)
            start_sum(step, 1, end_sum(step, 0))
            for piece in range(early, PIECES if step < ITERS - 1 else 0):
                start_halo(step + 1, piece)
            packed = end_sum(step, 1)
        norm, curve = packed[0:1, :], packed[1:2, :]
        if step > 0:
            betas.append(norm / norms[-1])
            curve = curve + betas[-1] * (packed[2:3, :] + betas[-1] * curves[-1])
        norms.append(norm)
        curves.append(curve)
        alphas.append(norm / curve)
        alpha, beta = alphas[-1], betas[-1]
        if step == ITERS - 1:
            coef_ref[...] = jnp.concatenate([alpha, beta, jnp.zeros((6, BS), jnp.float32)], axis=0)
            break

        def update(t, unused, step=step, alpha=alpha, beta=beta):
            r = res_ref[rows(t), :]
            dt, qt = r, w[rows(t), :]
            if step > 0:
                dt = dt + beta * d[rows(t), :]
                qt = qt + beta * q[rows(t), :]
            moved = alpha * dt
            sol_ref[rows(t), :] = moved if step == 0 else sol_ref[rows(t), :] + moved
            r = r - alpha * qt
            res_ref[rows(t), :] = r
            d[rows(t), :] = dt
            q[rows(t), :] = qt
            vec[step + 1, middle(t), :] = r.astype(jnp.bfloat16)
            return unused

        def update_halo(t, unused, step=step):
            for block in (t, 2 * ROWS + t):
                at = rows(block)
                shift = ridge[at, :]
                r = vec[0, at, :].astype(jnp.float32)
                move, push = r, pull[0, at, :].astype(jnp.float32)
                r = r - alphas[0] * (shift * move + push)
                if step > 0:
                    move = r + betas[1] * move
                    push = pull[1, at, :].astype(jnp.float32) + betas[1] * push
                    r = r - alphas[1] * (shift * move + push)
                vec[step + 1, at, :] = r.astype(jnp.bfloat16)
            return unused

        lax.fori_loop(0, ROWS, update, 0)
        end_halo(step + 1)
        lax.fori_loop(0, ROWS, update_halo, 0)

    for one in sent:
        one.wait_send()


def local(targets, ridge, blocks, col_index, row_length):
    slots = col_index.shape[1]
    size = ROWS * BS
    f32 = jnp.float32
    vmem = pl.BlockSpec(memory_space=pltpu.VMEM)
    hbm = pl.BlockSpec(memory_space=pltpu.HBM)
    kinds = PAIRS * 23
    field = jax.ShapeDtypeStruct((size, BS), f32)
    operands = (col_index, row_length, targets, ridge.reshape(ROWS, BS), blocks)
    solution, residual, d, q, w, coef = pl.pallas_call(
        kernel,
        out_shape=[field] * 5 + [jax.ShapeDtypeStruct((8, BS), f32)],
        in_specs=[hbm] * 5,
        out_specs=[vmem] * 6,
        scratch_shapes=[
            pltpu.SMEM((ROWS, slots), jnp.int32),
            pltpu.SMEM((ROWS,), jnp.int32),
            pltpu.SMEM((ROWS, BAND), jnp.int32),
            pltpu.VMEM((ROWS, slots, SUB, BS), jnp.bfloat16),
            pltpu.VMEM((PARTS, SUB, TILES * BS), jnp.bfloat16),
            pltpu.VMEM((ROWS, BS, 3 * size), jnp.bfloat16),
            pltpu.VMEM((ITERS, 3 * size, BS), jnp.bfloat16),
            pltpu.VMEM((ITERS - 1, 3 * size, BS), jnp.bfloat16),
            pltpu.VMEM((size, BS), f32),
            pltpu.VMEM((3, ROWS, BS), f32),
            pltpu.VMEM((3 * size, BS), f32),
            pltpu.VMEM((2 * ITERS, 8, BS), f32),
            pltpu.VMEM((2 * ITERS * (RING - 1), 8, BS), f32),
            pltpu.SemaphoreType.DMA((5,)),
            pltpu.SemaphoreType.DMA((kinds,)),
            pltpu.SemaphoreType.DMA((kinds,)),
            pltpu.SemaphoreType.DMA((2 * ITERS * PIECES + 2,)),
            pltpu.SemaphoreType.DMA((2 * ITERS * PIECES + 2,)),
            pltpu.SemaphoreType.DMA((2 * ITERS * (RING - 1),)),
            pltpu.SemaphoreType.DMA((2 * ITERS * (RING - 1),)),
        ],
        compiler_params=pltpu.CompilerParams(
            collective_id=0, has_side_effects=True, vmem_limit_bytes=36 * 2**20
        ),
    )(*(pltpu.with_memory_space_constraint(one, pltpu.HBM) for one in operands))
    alpha, beta = coef[0:1], coef[1:2]
    return solution + alpha * (residual + beta * d), residual - alpha * (w + beta * q)


def solution(mesh):
    return jax.shard_map(
        local,
        mesh=mesh,
        in_specs=(
            P("asset", "rhs"),
            P("asset"),
            P("asset", None, "rhs", None),
            P("asset", None),
            P("asset"),
        ),
        out_specs=(P("asset", "rhs"), P("asset", "rhs")),
        check_vma=False,
    )
```
